256 devices in a mesh: seq: 64 (over x, z, core), chan: 4 (over y).
Axes of the slice: x: 4, y: 4, z: 8, core: 2. Of those that a mesh axis runs over, the one named last changes fastest.
Arguments:
- signal: bfloat16 [8192, 4096], P('seq', 'chan'), may hold values from -6 to 6
- gate: bfloat16 [8192, 4096], P('seq', 'chan'), may hold values from -6 to 6
- curvature: bfloat16 [8192, 4096], P('seq', 'chan'), may hold values from -6 to 6
- filters: bfloat16 [8192, 8], P('seq'), may hold values from -0.0625 to 0.0625
- probe: int32 [8192, 8], P('seq'), may hold values from 0 to 1
- group_ids: int32 [4096], P('chan'), may hold values from 0 to 7
Outputs:
- gated_output: bfloat16 [8192, 4096], P('seq', 'chan')
- curvature_probe: bfloat16 [8192, 8], P('seq', 'chan')
The draws below stay inside these ranges and needn't reach their ends.
Inputs may be any that keep to these rules, and one draw needn't show every extreme that they name: The probe's sign at a tap is 2 * bit - 1.
All inputs are finite; a program needn't handle non-finite values.
Results may differ from the reference program's by a relative error of at most 0.014.
Values may be sent and summed in bfloat16 or wider, within the bound.
A program may use at most 64 MiB of HBM per device.

```python
import math
import jax
import jax.numpy as jnp
from jax import lax

C = 4096
G = 8
L = 8192


def with_ends(entries, key, low, high):
    extent = entries.shape
    place = [jax.random.randint(jax.random.fold_in(key, axis), (), 0, extent[axis]) for axis in range(len(extent))]
    entries = entries.at[tuple(place)].set(low)
    longest = extent.index(max(extent))
    place[longest] = (place[longest] + 1) % extent[longest]
    return entries.at[tuple(place)].set(high)


def block_levels(own_key, dims, cuts, smallest, largest):
    factor_of = 1.0
    for position, shards_of in cuts:
        steps = jax.random.uniform(jax.random.fold_in(jax.random.fold_in(own_key, 6), position), (shards_of,), jnp.float32, smallest / len(cuts), largest / len(cuts))
        factor_of = factor_of * jnp.repeat(jnp.exp(steps), dims[position] // shards_of).reshape((-1,) + (1,) * (len(dims) - 1 - position))
    return factor_of


def gaussian(key, extent, scale, bound, pieces=(), kind=jnp.bfloat16):
    gain = block_levels(key, extent, pieces, -0.22, 0.18) if pieces else 1.0
    entries = jax.random.normal(key, extent, jnp.float32) * scale * gain
    return jnp.minimum(jnp.maximum(entries, -bound), bound).astype(kind)


def setup_inputs(seed: int = 0) -> dict:
    streams_of = jax.random.split(jax.random.key(seed), 7)
    return {
        "signal": gaussian(streams_of[0], (L, C), 1.0, 6.0, ((0, 64), (1, 4))),
        "gate": gaussian(streams_of[1], (L, C), 1.0, 6.0, ((0, 64), (1, 4))),
        "curvature": gaussian(streams_of[2], (L, C), 1.0, 6.0, ((0, 64), (1, 4))),
        "filters": gaussian(streams_of[3], (L, G), L ** -0.5, 0.0625, ((0, 64),)),
        "probe": with_ends(jax.random.randint(streams_of[4], (L, G), 0, 2), jax.random.fold_in(streams_of[4], 1), 0, 1).astype(jnp.int32),
        "group_ids": with_ends(jax.random.randint(streams_of[5], (C,), 0, G), jax.random.fold_in(streams_of[5], 1), 0, G - 1).astype(jnp.int32),
    }


HIGHEST_PREC = lax.Precision.HIGHEST

def spectrum(values):
    padded = jnp.pad(values, ((0, values.shape[0]), (0, 0)))
    return jnp.fft.fft(padded, axis=0)

def reference(signal, gate, curvature, filters, probe, group_ids):
    filter_spec = spectrum(filters.astype(jnp.float32))
    probe_spec = spectrum((2 * probe - 1).astype(jnp.float32)) / math.sqrt(L)
    onehot = (group_ids[:, None] == jnp.arange(G, dtype=jnp.int32)[None, :]).astype(jnp.float32)
    block_width = math.gcd(C, 512)
    block_count = C // block_width

    def step_block(carry, block_index):
        sum_real, sum_imag = carry
        start = block_index * block_width
        sig_block = lax.dynamic_slice_in_dim(signal, start, block_width, 1).astype(jnp.float32)
        gate_float = lax.dynamic_slice_in_dim(gate, start, block_width, 1).astype(jnp.float32)
        curv_float = lax.dynamic_slice_in_dim(curvature, start, block_width, 1).astype(jnp.float32)
        ids_block = lax.dynamic_slice_in_dim(group_ids, start, block_width, 0)
        hot_block = lax.dynamic_slice_in_dim(onehot, start, block_width, 0)
        sig_spec = spectrum(sig_block)
        primal = jnp.fft.ifft(sig_spec * jnp.take(filter_spec, ids_block, axis=1), axis=0)[:L].real.astype(jnp.bfloat16)
        tangent = jnp.fft.ifft(sig_spec * jnp.take(probe_spec, ids_block, axis=1), axis=0)[:L].real.astype(jnp.bfloat16)
        output_mix = (gate_float * primal.astype(jnp.float32)).astype(jnp.bfloat16)
        weighted = (gate_float * gate_float * curv_float * tangent.astype(jnp.float32)).astype(jnp.bfloat16)
        back_spec = spectrum(weighted.astype(jnp.float32))
        product = jnp.conj(sig_spec) * back_spec
        sum_real = sum_real + jnp.dot(product.real, hot_block, precision=HIGHEST_PREC)
        sum_imag = sum_imag + jnp.dot(product.imag, hot_block, precision=HIGHEST_PREC)
        return ((sum_real, sum_imag), output_mix)
    zeros_init = jnp.zeros((2 * L, G), jnp.float32)
    totals, blocks = lax.scan(step_block, (zeros_init, zeros_init), jnp.arange(block_count, dtype=jnp.int32))
    gated_output = jnp.transpose(blocks, (1, 0, 2)).reshape(L, C)
    out_scale = 1.0 / math.sqrt(L * C / G)
    inverse_time = jnp.fft.ifft(totals[0] + 1j * totals[1], axis=0)[:L].real
    curvature_probe = (inverse_time * out_scale).astype(jnp.bfloat16)
    return (gated_output, curvature_probe)
```

```python
import functools
import math

import jax
import jax.numpy as jnp
import numpy as np
from jax import lax
from jax.experimental import pallas as pl
from jax.experimental.pallas import tpu as pltpu
from jax.sharding import PartitionSpec as P

SPAN = 128
HALF = 64
KEPT = 80
BF16 = jnp.bfloat16
F32 = jnp.float32


def tables():
    total = SPAN * SPAN
    k2 = np.arange(KEPT)
    live = (k2 <= SPAN // 2).astype(np.float64)
    n1 = np.arange(HALF)
    outer = 2 * np.pi * (np.outer(k2, n1) % SPAN) / SPAN
    enter = np.concatenate([np.cos(outer) * live[:, None], -np.sin(outer) * live[:, None]])
    weight = live * np.where((k2 == 0) | (k2 == SPAN // 2), 1.0, 2.0)
    leave = np.concatenate([(np.cos(outer) * weight[:, None]).T, (-np.sin(outer) * weight[:, None]).T], axis=1)
    fine = np.arange(SPAN)
    twist = 2 * np.pi * np.outer(k2, fine) / total
    turn = np.concatenate([np.cos(twist), np.sin(twist)], axis=1)
    inner = 2 * np.pi * (np.outer(fine, fine) % SPAN) / SPAN
    cos, sin = np.cos(inner), np.sin(inner)
    ahead = np.block([[cos, -sin], [sin, cos]])
    back = np.block([[cos, sin], [-sin, cos]])
    cast = lambda a: a.astype(np.float32).astype(BF16)
    return cast(enter), cast(leave), turn.astype(np.float32), cast(ahead), cast(back)


def dot(a, b):
    return jnp.dot(a, b, preferred_element_type=F32)


def spread_columns(src, wide, cols):
    width = src.shape[1]
    wide[...] = src[...].astype(F32).reshape(HALF * width, SPAN)
    for c in range(width):
        cols[:, c * SPAN : (c + 1) * SPAN] = wide[pl.ds(c, HALF, stride=width), :].astype(BF16)


def forward(cols, enter, turn, ahead, rows, spec):
    width = spec.shape[0]
    tc, ts = turn[:, :SPAN], turn[:, SPAN:]
    for q in range(0, width, 4):
        mixed = dot(enter[...], cols[:, q * SPAN : (q + 4) * SPAN])
        for c in range(4):
            re = mixed[:KEPT, c * SPAN : (c + 1) * SPAN]
            im = mixed[KEPT:, c * SPAN : (c + 1) * SPAN]
            r0 = (q + c) * KEPT
            rows[r0 : r0 + KEPT, :SPAN] = (re * tc + im * ts).astype(BF16)
            rows[r0 : r0 + KEPT, SPAN:] = (im * tc - re * ts).astype(BF16)
    for q in range(0, width, 4):
        spec[q : q + 4] = dot(rows[q * KEPT : (q + 4) * KEPT, :], ahead[...]).reshape(4, KEPT, 2 * SPAN)


def untwist(block, tc, ts):
    re, im = block[:, :SPAN], block[:, SPAN:]
    return jnp.concatenate([re * tc - im * ts, im * tc + re * ts], axis=0).astype(BF16)


def transform_body(sig, taps, mix, gid, enter, leave, turn, ahead, back, prim, part,
                   wide, cols, rows, sig_spec, tap_spec, back_spec, group_spec):
    width = sig.shape[1]
    groups = tap_spec.shape[0] // 2
    total = SPAN * SPAN
    probe_scale = 1.0 / math.sqrt(HALF * SPAN)
    tc, ts = turn[:, :SPAN], turn[:, SPAN:]
    spread_columns(sig, wide, cols)
    forward(cols, enter, turn, ahead, rows, sig_spec)
    spread_columns(taps, wide, cols)
    forward(cols, enter, turn, ahead, rows, tap_spec)
    wide[...] = mix[...].astype(F32).reshape(HALF * width, SPAN)
    for c in range(width):
        g = gid[c]
        sr, si = sig_spec[c, :, :SPAN], sig_spec[c, :, SPAN:]
        for kind in range(2):
            fr, fi = tap_spec[g + kind * groups, :, :SPAN], tap_spec[g + kind * groups, :, SPAN:]
            r0 = kind * KEPT
            rows[r0 : r0 + KEPT, :SPAN] = (sr * fr - si * fi).astype(BF16)
            rows[r0 : r0 + KEPT, SPAN:] = (sr * fi + si * fr).astype(BF16)
        inner = dot(rows[: 2 * KEPT, :], back[...])
        both = jnp.concatenate([untwist(inner[:KEPT], tc, ts), untwist(inner[KEPT:], tc, ts)], axis=1)
        timed = dot(leave[...], both)
        weight = wide[pl.ds(c, HALF, stride=width), :]
        wide[pl.ds(c, HALF, stride=width), :] = timed[:, :SPAN] * (1.0 / total)
        tangent = (timed[:, SPAN:] * (probe_scale / total)).astype(BF16).astype(F32)
        cols[:, c * SPAN : (c + 1) * SPAN] = (tangent * weight).astype(BF16)
    prim[...] = wide[...].astype(BF16).reshape(prim.shape)
    forward(cols, enter, turn, ahead, rows, back_spec)
    for c in range(width):
        sr, si = sig_spec[c, :, :SPAN], sig_spec[c, :, SPAN:]
        br, bi = back_spec[c, :, :SPAN], back_spec[c, :, SPAN:]
        back_spec[c] = jnp.concatenate([sr * br + si * bi, sr * bi - si * br], axis=1)
    for g in range(groups):
        acc = jnp.zeros((KEPT, 2 * SPAN), F32)
        for c in range(width):
            acc = acc + jnp.where(gid[c] == g, 1.0, 0.0).astype(F32) * back_spec[c]
        group_spec[g * KEPT : (g + 1) * KEPT, :] = acc.astype(BF16)
    for g in range(0, groups, 2):
        inner = dot(group_spec[g * KEPT : (g + 2) * KEPT, :], back[...])
        both = jnp.concatenate([untwist(inner[:KEPT], tc, ts), untwist(inner[KEPT:], tc, ts)], axis=1)
        timed = dot(leave[...], both)
        part[g] = timed[:, :SPAN]
        part[g + 1] = timed[:, SPAN:]


def transform(sig, taps, mix, gid, groups):
    width = sig.shape[1]
    vmem = pl.BlockSpec(memory_space=pltpu.VMEM)
    return pl.pallas_call(
        transform_body,
        out_shape=(
            jax.ShapeDtypeStruct(sig.shape, BF16),
            jax.ShapeDtypeStruct((groups, HALF, SPAN), F32),
        ),
        in_specs=[vmem] * 3 + [pl.BlockSpec(memory_space=pltpu.SMEM)] + [vmem] * 5,
        out_specs=(vmem, vmem),
        scratch_shapes=[
            pltpu.VMEM((HALF * width, SPAN), F32),
            pltpu.VMEM((HALF, width * SPAN), BF16),
            pltpu.VMEM((width * KEPT, 2 * SPAN), BF16),
            pltpu.VMEM((width, KEPT, 2 * SPAN), F32),
            pltpu.VMEM((2 * groups, KEPT, 2 * SPAN), F32),
            pltpu.VMEM((width, KEPT, 2 * SPAN), F32),
            pltpu.VMEM((groups * KEPT, 2 * SPAN), BF16),
        ],
        compiler_params=pltpu.CompilerParams(vmem_limit_bytes=40 << 20),
    )(sig, taps, mix, gid, *[jnp.asarray(t) for t in tables()])


def local(signal, gate, curvature, filters, probe, group_ids):
    devices = lax.axis_size("seq")
    position = lax.axis_index("seq")
    seq_rows, chan_width = signal.shape
    groups = filters.shape[1]
    width = chan_width // devices
    gate_float = gate.astype(F32)
    mix = (gate_float * gate_float * curvature.astype(F32)).astype(BF16)
    taps = jnp.concatenate([filters, (2 * probe - 1).astype(BF16)], axis=1).T
    tiled = lambda a: a.T.reshape(devices, width, seq_rows)
    sent = jnp.stack([tiled(signal), jnp.broadcast_to(taps[None], (devices, width, seq_rows)), tiled(mix)], axis=1)
    got = lax.all_to_all(sent, "seq", split_axis=0, concat_axis=0, tiled=True)
    own = lax.dynamic_slice_in_dim(group_ids, position * width, width, 0)
    prim, part = transform(got[:, 0], got[:, 1], got[:, 2], own, groups)
    home = lax.all_to_all(prim, "seq", split_axis=0, concat_axis=0, tiled=True)
    output_mix = (gate_float * home.reshape(chan_width, seq_rows).T.astype(F32)).astype(BF16)
    summed = lax.psum_scatter(part, "chan", scatter_dimension=0, tiled=True)
    summed = lax.psum_scatter(summed, "seq", scatter_dimension=1, tiled=True)
    length = seq_rows * devices
    total_width = chan_width * lax.axis_size("chan")
    scale = 1.0 / (math.sqrt(length * total_width / groups) * SPAN * SPAN)
    return (output_mix, (summed[:, 0, :].T * scale).astype(BF16))


def solution(mesh):
    return jax.shard_map(
        local,
        mesh=mesh,
        in_specs=(
            P("seq", "chan"),
            P("seq", "chan"),
            P("seq", "chan"),
            P("seq", None),
            P("seq", None),
            P("chan"),
        ),
        out_specs=(P("seq", "chan"), P("seq", "chan")),
        check_vma=False,
    )
```

```python
import math

import jax
import jax.numpy as jnp
import numpy as np
from jax import lax
from jax.experimental import pallas as pl
from jax.experimental.pallas import tpu as pltpu
from jax.sharding import PartitionSpec as P

SPAN = 128
HALF = 64
KEPT = 80
BF16 = jnp.bfloat16
F32 = jnp.float32
MESH = pl.DeviceIdType.MESH


def tables():
    total = SPAN * SPAN
    k2 = np.arange(KEPT)
    live = (k2 <= SPAN // 2).astype(np.float64)
    n1 = np.arange(HALF)
    outer = 2 * np.pi * (np.outer(k2, n1) % SPAN) / SPAN
    enter = np.concatenate([np.cos(outer) * live[:, None], -np.sin(outer) * live[:, None]])
    weight = live * np.where((k2 == 0) | (k2 == SPAN // 2), 1.0, 2.0)
    leave = np.concatenate([(np.cos(outer) * weight[:, None]).T, (-np.sin(outer) * weight[:, None]).T], axis=1)
    fine = np.arange(SPAN)
    twist = 2 * np.pi * np.outer(k2, fine) / total
    turn = np.concatenate([np.cos(twist), np.sin(twist)], axis=1)
    inner = 2 * np.pi * (np.outer(fine, fine) % SPAN) / SPAN
    cos, sin = np.cos(inner), np.sin(inner)
    ahead = np.block([[cos, -sin], [sin, cos]])
    back = np.block([[cos, sin], [-sin, cos]])
    cast = lambda a: a.astype(np.float32).astype(BF16)
    return cast(enter), cast(leave), turn.astype(np.float32), cast(ahead), cast(back)


def dot(a, b):
    return jnp.dot(a, b, preferred_element_type=F32)


def spread_columns(src, wide, cols):
    width = src.shape[1]
    wide[...] = src[...].astype(F32).reshape(HALF * width, SPAN)
    for c in range(width):
        cols[:, c * SPAN : (c + 1) * SPAN] = wide[pl.ds(c, HALF, stride=width), :].astype(BF16)


def forward(cols, enter, turn, ahead, rows, spec):
    width = spec.shape[0]
    tc, ts = turn[:, :SPAN], turn[:, SPAN:]
    for q in range(0, width, 4):
        mixed = dot(enter[...], cols[:, q * SPAN : (q + 4) * SPAN])
        for c in range(4):
            re = mixed[:KEPT, c * SPAN : (c + 1) * SPAN]
            im = mixed[KEPT:, c * SPAN : (c + 1) * SPAN]
            r0 = (q + c) * KEPT
            rows[r0 : r0 + KEPT, :SPAN] = (re * tc + im * ts).astype(BF16)
            rows[r0 : r0 + KEPT, SPAN:] = (im * tc - re * ts).astype(BF16)
    for q in range(0, width, 4):
        spec[q : q + 4] = dot(rows[q * KEPT : (q + 4) * KEPT, :], ahead[...]).reshape(4, KEPT, 2 * SPAN)


def untwist(block, tc, ts):
    re, im = block[:, :SPAN], block[:, SPAN:]
    return jnp.concatenate([re * tc - im * ts, im * tc + re * ts], axis=0).astype(BF16)


def tiles_of(block):
    return block.astype(F32).T.astype(BF16)


def body(signal, gate, curvature, filters, probe, gid, enter, leave, turn, ahead, back, gated, curved,
         sig_out, sig_in, tap_out, tap_in, mix_out, mix_in, prim_out, home, part_out, part_in, sum_out, sum_in,
         wide, cols, rows, sig_spec, tap_spec, back_spec, group_spec, send, recv):
    me = lax.axis_index("seq")
    lane = lax.axis_index("chan")
    peers = lax.axis_size("seq")
    lanes = lax.axis_size("chan")
    width = sig_in.shape[1]
    chans = width * peers
    groups = filters.shape[0]
    total = SPAN * SPAN
    probe_scale = 1.0 / math.sqrt(HALF * SPAN)
    tc, ts = turn[:, :SPAN], turn[:, SPAN:]

    barrier = pltpu.get_barrier_semaphore()

    @pl.loop(1, peers)
    def _(k):
        pl.semaphore_signal(barrier, inc=1, device_id={"seq": lax.rem(me + k, peers)}, device_id_type=MESH)

    for k in range(1, lanes):
        pl.semaphore_signal(barrier, inc=1, device_id={"chan": lax.rem(lane + k, lanes)}, device_id_type=MESH)

    per = SPAN // width
    for b in range(chans // SPAN):
        sig_out[b * per : (b + 1) * per] = tiles_of(signal[:, b * SPAN : (b + 1) * SPAN]).reshape(per, width, SPAN)
    signs = 2.0 * probe[...].astype(F32) - 1.0
    tap_out[...] = jnp.concatenate([filters[...].astype(F32), signs], axis=0).astype(BF16)
    sig_in[me] = sig_out[me]
    tap_in[me] = tap_out[...]
    pl.semaphore_wait(barrier, peers + lanes - 2)

    def tile_copy(slot, src, dst, to):
        return pltpu.make_async_remote_copy(
            src_ref=src, dst_ref=dst, send_sem=send.at[slot], recv_sem=recv.at[slot],
            device_id={"seq": to}, device_id_type=MESH,
        )

    def scatter(slot, out, into):
        @pl.loop(1, peers)
        def _(k):
            to = lax.rem(me + k, peers)
            tile_copy(slot, out.at[to], into.at[me], to).start()

    def whole(slot, out, into):
        rest = pl.ds(0, peers - 1)
        return tile_copy(slot, out.at[rest], into.at[rest], lax.rem(me + 1, peers))

    scatter(0, sig_out, sig_in)

    @pl.loop(1, peers)
    def _(k):
        to = lax.rem(me + k, peers)
        tile_copy(1, tap_out, tap_in.at[me], to).start()

    for b in range(chans // SPAN):
        g32 = gate[:, b * SPAN : (b + 1) * SPAN].astype(F32)
        mixed = g32 * g32 * curvature[:, b * SPAN : (b + 1) * SPAN].astype(F32)
        mix_out[b * per : (b + 1) * per] = tiles_of(mixed).reshape(per, width, SPAN)
    mix_in[me] = mix_out[me]
    scatter(2, mix_out, mix_in)

    whole(0, sig_out, sig_in).wait_recv()
    spread_columns(sig_in, wide, cols)
    forward(cols, enter, turn, ahead, rows, sig_spec)
    whole(1, mix_out, tap_in).wait_recv()
    spread_columns(tap_in, wide, cols)
    forward(cols, enter, turn, ahead, rows, tap_spec)
    whole(2, mix_out, mix_in).wait_recv()
    wide[...] = mix_in[...].astype(F32).reshape(HALF * width, SPAN)
    for c in range(width):
        g = gid[me * width + c]
        sr, si = sig_spec[c, :, :SPAN], sig_spec[c, :, SPAN:]
        for kind in range(2):
            taps = tap_spec[g + kind * groups]
            fr, fi = taps[:, :SPAN], taps[:, SPAN:]
            r0 = (2 * c + kind) * KEPT
            rows[r0 : r0 + KEPT, :SPAN] = (sr * fr - si * fi).astype(BF16)
            rows[r0 : r0 + KEPT, SPAN:] = (sr * fi + si * fr).astype(BF16)
        inner = dot(rows[2 * c * KEPT : 2 * (c + 1) * KEPT, :], back[...])
        both = jnp.concatenate([untwist(inner[:KEPT], tc, ts), untwist(inner[KEPT:], tc, ts)], axis=1)
        timed = dot(leave[...], both)
        weight = wide[pl.ds(c, HALF, stride=width), :]
        wide[pl.ds(c, HALF, stride=width), :] = timed[:, :SPAN] * (1.0 / total)
        tangent = (timed[:, SPAN:] * (probe_scale / total)).astype(BF16).astype(F32)
        cols[:, c * SPAN : (c + 1) * SPAN] = (tangent * weight).astype(BF16)
    prim_out[...] = wide[...].astype(BF16).reshape(prim_out.shape)
    home[me] = prim_out[me]
    scatter(3, prim_out, home)

    forward(cols, enter, turn, ahead, rows, back_spec)
    for c in range(width):
        sr, si = sig_spec[c, :, :SPAN], sig_spec[c, :, SPAN:]
        br, bi = back_spec[c, :, :SPAN], back_spec[c, :, SPAN:]
        back_spec[c] = jnp.concatenate([sr * br + si * bi, sr * bi - si * br], axis=1)
    for g in range(groups):
        acc = jnp.zeros((KEPT, 2 * SPAN), F32)
        for c in range(width):
            acc = acc + jnp.where(gid[me * width + c] == g, 1.0, 0.0).astype(F32) * back_spec[c]
        group_spec[g * KEPT : (g + 1) * KEPT, :] = acc.astype(BF16)
    for g in range(0, groups, 2):
        inner = dot(group_spec[g * KEPT : (g + 2) * KEPT, :], back[...])
        both = jnp.concatenate([untwist(inner[:KEPT], tc, ts), untwist(inner[KEPT:], tc, ts)], axis=1)
        timed = dot(leave[...], both)
        wide[pl.ds(g, HALF, stride=groups), :] = timed[:, :SPAN]
        wide[pl.ds(g + 1, HALF, stride=groups), :] = timed[:, SPAN:]
    part_out[...] = wide[: HALF * groups, :].reshape(part_out.shape)
    part_in[me] = part_out[me]
    scatter(4, part_out, part_in)

    whole(3, prim_out, home).wait_recv()
    for b in range(chans // SPAN):
        block = home[b * per : (b + 1) * per].reshape(SPAN, SPAN)
        lot = slice(b * SPAN, (b + 1) * SPAN)
        gated[:, lot] = (gate[:, lot].astype(F32) * block.astype(F32).T).astype(BF16)

    whole(4, part_out, part_in).wait_recv()
    sum_out[...] = jnp.sum(part_in[...], axis=0)
    sum_in[lane] = sum_out[...]
    gathers = []
    for k in range(1, lanes):
        to = lax.rem(lane + k, lanes)
        copy = pltpu.make_async_remote_copy(
            src_ref=sum_out, dst_ref=sum_in.at[lane], send_sem=send.at[4 + k], recv_sem=recv.at[4 + k],
            device_id={"chan": to}, device_id_type=MESH,
        )
        copy.start()
        gathers.append(copy)
    whole(0, sig_out, sig_in).wait_send()
    whole(1, sig_out, sig_in).wait_send()
    whole(2, mix_out, mix_in).wait_send()
    whole(3, prim_out, home).wait_send()
    whole(4, part_out, part_in).wait_send()
    for copy in gathers:
        copy.wait()
    scale = 1.0 / (math.sqrt(HALF * SPAN * chans * lanes / groups) * total)
    curved[...] = jnp.sum(sum_in[...], axis=0) * scale


def local(signal, gate, curvature, filters, probe, group_ids):
    peers, lanes = lax.axis_size("seq"), lax.axis_size("chan")
    seq_rows, chans = signal.shape
    groups = filters.shape[1]
    width = chans // peers
    vmem = pl.BlockSpec(memory_space=pltpu.VMEM)
    tile = pltpu.VMEM((peers, width, seq_rows), BF16)
    output_mix, curved = pl.pallas_call(
        body,
        out_shape=(
            jax.ShapeDtypeStruct((seq_rows, chans), BF16),
            jax.ShapeDtypeStruct((groups, seq_rows), F32),
        ),
        in_specs=[vmem] * 5 + [pl.BlockSpec(memory_space=pltpu.SMEM)] + [vmem] * 5,
        out_specs=(vmem, vmem),
        scratch_shapes=[
            tile,
            tile,
            pltpu.VMEM((width, seq_rows), BF16),
            tile,
            tile,
            tile,
            tile,
            tile,
            pltpu.VMEM((peers, groups, seq_rows), F32),
            pltpu.VMEM((peers, groups, seq_rows), F32),
            pltpu.VMEM((groups, seq_rows), F32),
            pltpu.VMEM((lanes, groups, seq_rows), F32),
            pltpu.VMEM((HALF * width, SPAN), F32),
            pltpu.VMEM((HALF, width * SPAN), BF16),
            pltpu.VMEM((2 * width * KEPT, 2 * SPAN), BF16),
            pltpu.VMEM((width, KEPT, 2 * SPAN), F32),
            pltpu.VMEM((2 * groups, KEPT, 2 * SPAN), F32),
            pltpu.VMEM((width, KEPT, 2 * SPAN), F32),
            pltpu.VMEM((groups * KEPT, 2 * SPAN), BF16),
            pltpu.SemaphoreType.DMA((4 + lanes,)),
            pltpu.SemaphoreType.DMA((4 + lanes,)),
        ],
        compiler_params=pltpu.CompilerParams(
            collective_id=0, has_side_effects=True, vmem_limit_bytes=40 << 20
        ),
    )(signal, gate, curvature, filters.T, probe.T, group_ids, *[jnp.asarray(t) for t in tables()])
    share = groups // lanes
    mine = lax.dynamic_slice_in_dim(curved, lax.axis_index("chan") * share, share, 0)
    return (output_mix, mine.T.astype(BF16))


def solution(mesh):
    return jax.shard_map(
        local,
        mesh=mesh,
        in_specs=(
            P("seq", "chan"),
            P("seq", "chan"),
            P("seq", "chan"),
            P("seq", None),
            P("seq", None),
            P("chan"),
        ),
        out_specs=(P("seq", "chan"), P("seq", "chan")),
        check_vma=False,
    )
```

```python
import math

import jax
import jax.numpy as jnp
import numpy as np
from jax import lax
from jax.experimental import pallas as pl
from jax.experimental.pallas import tpu as pltpu
from jax.sharding import PartitionSpec as P

SPAN = 128
HALF = 64
KEPT = 80
BF16 = jnp.bfloat16
F32 = jnp.float32
MESH = pl.DeviceIdType.MESH
DEPTH = 8
CORES = 2


def tables():
    total = SPAN * SPAN
    k2 = np.arange(KEPT)
    live = (k2 <= SPAN // 2).astype(np.float64)
    n1 = np.arange(HALF)
    outer = 2 * np.pi * (np.outer(k2, n1) % SPAN) / SPAN
    enter = np.concatenate([np.cos(outer) * live[:, None], -np.sin(outer) * live[:, None]])
    weight = live * np.where((k2 == 0) | (k2 == SPAN // 2), 1.0, 2.0)
    leave = np.concatenate([(np.cos(outer) * weight[:, None]).T, (-np.sin(outer) * weight[:, None]).T], axis=1)
    fine = np.arange(SPAN)
    twist = 2 * np.pi * np.outer(k2, fine) / total
    turn = np.concatenate([np.cos(twist), np.sin(twist)], axis=1)
    inner = 2 * np.pi * (np.outer(fine, fine) % SPAN) / SPAN
    cos, sin = np.cos(inner), np.sin(inner)
    ahead = np.block([[cos, -sin], [sin, cos]])
    back = np.block([[cos, sin], [-sin, cos]])
    cast = lambda a: a.astype(np.float32).astype(BF16)
    return cast(enter), cast(leave), turn.astype(np.float32), cast(ahead), cast(back)


def dot(a, b):
    return jnp.dot(a, b, preferred_element_type=F32)


def spread_columns(src, width, wide, cols):
    wide[...] = src[...].astype(F32).reshape(HALF * width, SPAN)
    for c in range(width):
        cols[:, c * SPAN : (c + 1) * SPAN] = wide[pl.ds(c, HALF, stride=width), :].astype(BF16)


def forward(cols, enter, turn, ahead, rows, spec):
    width = spec.shape[0]
    tc, ts = turn[:, :SPAN], turn[:, SPAN:]
    for q in range(0, width, 4):
        mixed = dot(enter[...], cols[:, q * SPAN : (q + 4) * SPAN])
        for c in range(4):
            re = mixed[:KEPT, c * SPAN : (c + 1) * SPAN]
            im = mixed[KEPT:, c * SPAN : (c + 1) * SPAN]
            r0 = (q + c) * KEPT
            rows[r0 : r0 + KEPT, :SPAN] = (re * tc + im * ts).astype(BF16)
            rows[r0 : r0 + KEPT, SPAN:] = (im * tc - re * ts).astype(BF16)
    for q in range(0, width, 4):
        spec[q : q + 4] = dot(rows[q * KEPT : (q + 4) * KEPT, :], ahead[...]).reshape(4, KEPT, 2 * SPAN)


def untwist(block, tc, ts):
    re, im = block[:, :SPAN], block[:, SPAN:]
    return jnp.concatenate([re * tc - im * ts, im * tc + re * ts], axis=0).astype(BF16)


def tiles_of(block):
    return block.astype(F32).T.astype(BF16)


def body(signal_hbm, gate_hbm, curvature_hbm, filters_hbm, probe_hbm, gid_hbm,
         enter_hbm, leave_hbm, regroup_hbm, turn_hbm, ahead_hbm, back_hbm, gated, curved,
         signal, gate, curvature, filters, probe, gid, enter, leave, regroup, turn, ahead, back,
         sig_out, sig_in, tap_in, mix_out, mix_in, prim_out, home, part_out, part_in, sum_out, sum_in,
         wide, tang, cols, rows, sig_spec, tap_spec, back_spec, group_spec, send, recv, load):
    me = lax.axis_index("seq")
    lane = lax.axis_index("chan")
    peers = lax.axis_size("seq")
    lanes = lax.axis_size("chan")
    near_z, near_x = me // CORES % DEPTH, me // (CORES * DEPTH)
    core = me % CORES
    across = peers // (CORES * DEPTH)
    column = across * CORES
    width = sig_in.shape[1]
    chans = width * peers
    groups = filters.shape[0]
    total = SPAN * SPAN
    probe_scale = 1.0 / math.sqrt(HALF * SPAN)

    def seq_of(x, z, half):
        return (x * DEPTH + z) * CORES + half

    loads = [
        pltpu.make_async_copy(src, dst, load.at[i])
        for i, (src, dst) in enumerate([
            (signal_hbm, signal), (filters_hbm, filters), (probe_hbm, probe), (gate_hbm, gate),
            (curvature_hbm, curvature), (enter_hbm, enter), (turn_hbm, turn), (ahead_hbm, ahead),
            (back_hbm, back), (leave_hbm, leave), (regroup_hbm, regroup), (gid_hbm, gid),
        ])
    ]
    for copy in loads:
        copy.start()

    barrier = pltpu.get_barrier_semaphore()

    @pl.loop(1, peers)
    def _(k):
        pl.semaphore_signal(barrier, inc=1, device_id={"seq": lax.rem(me + k, peers)}, device_id_type=MESH)

    def mate(k):
        x = lax.rem(near_x + k // CORES, across)
        return seq_of(x, near_z, lax.rem(core + k, CORES))

    @pl.loop(column, column * lanes)
    def _(k):
        to = {"seq": mate(k % column), "chan": lax.rem(lane + k // column, lanes)}
        pl.semaphore_signal(barrier, inc=1, device_id=to, device_id_type=MESH)

    per = SPAN // width
    loads[0].wait()
    for b in range(chans // SPAN):
        sig_out[b * per : (b + 1) * per] = tiles_of(signal[:, b * SPAN : (b + 1) * SPAN]).reshape(per, width, SPAN)
    sig_in[me] = sig_out[me]
    loads[1].wait()
    loads[2].wait()
    signs = 2.0 * probe[...].astype(F32) - 1.0
    tap_in[near_x, near_z, core] = jnp.concatenate([filters[...].astype(F32), signs], axis=0).astype(BF16)
    loads[3].wait()
    loads[4].wait()
    for b in range(chans // SPAN):
        g32 = gate[:, b * SPAN : (b + 1) * SPAN].astype(F32)
        mixed = g32 * g32 * curvature[:, b * SPAN : (b + 1) * SPAN].astype(F32)
        mix_out[b * per : (b + 1) * per] = tiles_of(mixed).reshape(per, width, SPAN)
    mix_in[me] = mix_out[me]
    pl.semaphore_wait(barrier, peers - 1 + column * (lanes - 1))

    def put(slot, src, dst, to):
        return pltpu.make_async_remote_copy(
            src_ref=src, dst_ref=dst, send_sem=send.at[slot], recv_sem=recv.at[slot],
            device_id=to, device_id_type=MESH,
        )

    def scatter(slot, out, into):
        @pl.loop(1, peers)
        def _(k):
            to = lax.rem(me + k, peers)
            put(slot, out.at[to], into.at[me], {"seq": to}).start()

    def lot(slot, ref, count):
        part = ref.at[pl.ds(0, count)]
        return put(slot, part, part, {"seq": lax.rem(me + 1, peers)})

    own_tap = tap_in.at[near_x, near_z, core]

    @pl.loop(1, DEPTH)
    def _(k):
        put(0, own_tap, own_tap, {"seq": seq_of(near_x, lax.rem(near_z + k, DEPTH), core)}).start()

    scatter(2, sig_out, sig_in)
    lot(0, sig_in, DEPTH - 1).wait_recv()
    own_line = tap_in.at[near_x, :, core]

    @pl.loop(1, column)
    def _(k):
        put(1, own_line, own_line, {"seq": mate(k)}).start()

    scatter(3, mix_out, mix_in)
    for copy in loads[5:]:
        copy.wait()
    tc, ts = turn[:, :SPAN], turn[:, SPAN:]

    lot(1, sig_in, DEPTH * (column - 1)).wait_recv()
    spread_columns(tap_in, width, wide, cols)
    forward(cols, enter, turn, ahead, rows, tap_spec)
    lot(2, sig_in, peers - 1).wait_recv()
    spread_columns(sig_in, width, wide, cols)
    forward(cols, enter, turn, ahead, rows, sig_spec)
    for c in range(width):
        g = gid[me * width + c]
        sr, si = sig_spec[c, :, :SPAN], sig_spec[c, :, SPAN:]
        for kind in range(2):
            taps = tap_spec[g + kind * groups]
            fr, fi = taps[:, :SPAN], taps[:, SPAN:]
            r0 = (2 * c + kind) * KEPT
            rows[r0 : r0 + KEPT, :SPAN] = (sr * fr - si * fi).astype(BF16)
            rows[r0 : r0 + KEPT, SPAN:] = (sr * fi + si * fr).astype(BF16)
        inner = dot(rows[2 * c * KEPT : 2 * (c + 1) * KEPT, :], back[...])
        both = jnp.concatenate([untwist(inner[:KEPT], tc, ts), untwist(inner[KEPT:], tc, ts)], axis=1)
        timed = dot(leave[...], both)
        wide[pl.ds(c, HALF, stride=width), :] = timed[:, :SPAN] * (1.0 / total)
        tang[c] = timed[:, SPAN:] * (probe_scale / total)
    prim_out[...] = wide[...].astype(BF16).reshape(prim_out.shape)
    home[me] = prim_out[me]
    scatter(4, prim_out, home)

    lot(3, mix_in, peers - 1).wait_recv()
    wide[...] = mix_in[...].astype(F32).reshape(HALF * width, SPAN)
    for c in range(width):
        tangent = tang[c].astype(BF16).astype(F32)
        cols[:, c * SPAN : (c + 1) * SPAN] = (tangent * wide[pl.ds(c, HALF, stride=width), :]).astype(BF16)
    forward(cols, enter, turn, ahead, rows, back_spec)
    for c in range(width):
        sr, si = sig_spec[c, :, :SPAN], sig_spec[c, :, SPAN:]
        br, bi = back_spec[c, :, :SPAN], back_spec[c, :, SPAN:]
        back_spec[c] = jnp.concatenate([sr * br + si * bi, sr * bi - si * br], axis=1)
    for g in range(groups):
        acc = jnp.zeros((KEPT, 2 * SPAN), F32)
        for c in range(width):
            acc = acc + jnp.where(gid[me * width + c] == g, 1.0, 0.0).astype(F32) * back_spec[c]
        group_spec[g * KEPT : (g + 1) * KEPT, :] = acc.astype(BF16)
    share = groups // lanes
    for g in range(0, groups, share):
        inner = dot(group_spec[g * KEPT : (g + share) * KEPT, :], back[...])
        both = jnp.concatenate([untwist(inner[i * KEPT : (i + 1) * KEPT], tc, ts) for i in range(share)], axis=1)
        timed = dot(regroup[...], both)
        for i in range(share):
            block = timed[:, i * SPAN : (i + 1) * SPAN].reshape(column, DEPTH, SPAN)
            part_out[g // share * column : (g // share + 1) * column, i * DEPTH : (i + 1) * DEPTH] = block
    mine = lane * column + near_x * CORES + core
    part_in[mine] = part_out[mine]

    @pl.loop(1, column * lanes)
    def _(k):
        seq, chan = mate(k % column), lax.rem(lane + k // column, lanes)
        slot = chan * column + (seq // (CORES * DEPTH)) * CORES + seq % CORES
        put(5, part_out.at[slot], part_in.at[mine], {"seq": seq, "chan": chan}).start()

    lot(4, home, peers - 1).wait_recv()
    for b in range(chans // SPAN):
        block = home[b * per : (b + 1) * per].reshape(SPAN, SPAN)
        span = slice(b * SPAN, (b + 1) * SPAN)
        gated[:, span] = (gate[:, span].astype(F32) * block.astype(F32).T).astype(BF16)

    lot(5, part_in, column * lanes - 1).wait_recv()
    summed = jnp.sum(part_in[...], axis=0)
    sum_out[...] = jnp.zeros_like(sum_out)
    for i in range(share):
        sum_out[pl.ds(i, DEPTH, stride=8), :] = summed[i * DEPTH : (i + 1) * DEPTH]
    sum_in[near_z] = sum_out[pl.ds(pl.multiple_of(near_z * 8, 8), 8), :]

    @pl.loop(1, DEPTH)
    def _(k):
        z = lax.rem(near_z + k, DEPTH)
        src = sum_out.at[pl.ds(pl.multiple_of(z * 8, 8), 8)]
        put(6, src, sum_in.at[near_z], {"seq": seq_of(near_x, z, core)}).start()

    lot(0, sig_out, DEPTH - 1).wait_send()
    lot(1, sig_out, DEPTH * (column - 1)).wait_send()
    lot(2, sig_out, peers - 1).wait_send()
    lot(3, mix_out, peers - 1).wait_send()
    lot(4, prim_out, peers - 1).wait_send()
    lot(5, part_out, column * lanes - 1).wait_send()
    lot(6, sum_in, DEPTH - 1).wait()
    scale = 1.0 / (math.sqrt(HALF * SPAN * chans * lanes / groups) * total)
    curved[...] = (jnp.sum(sum_in[...], axis=0)[:share] * scale).astype(BF16)


def local(signal, gate, curvature, filters, probe, group_ids):
    peers, lanes = lax.axis_size("seq"), lax.axis_size("chan")
    seq_rows, chans = signal.shape
    groups = filters.shape[1]
    width = chans // peers
    across = peers // (CORES * DEPTH)
    column = across * CORES
    vmem = pl.BlockSpec(memory_space=pltpu.VMEM)
    hbm = pl.BlockSpec(memory_space=pltpu.HBM)
    tile = pltpu.VMEM((peers, width, seq_rows), BF16)
    inputs = [signal, gate, curvature, filters.T, probe.T, group_ids]
    enter, leave, turn, ahead, back = tables()
    order = np.arange(peers).reshape(across, DEPTH, CORES).transpose(0, 2, 1).reshape(-1)
    inputs += [jnp.asarray(t) for t in (enter, leave, leave[order], turn, ahead, back)]
    output_mix, curved = pl.pallas_call(
        body,
        out_shape=(
            jax.ShapeDtypeStruct((seq_rows, chans), BF16),
            jax.ShapeDtypeStruct((groups // lanes, seq_rows), BF16),
        ),
        in_specs=[hbm] * len(inputs),
        out_specs=(vmem, vmem),
        scratch_shapes=[
            (pltpu.SMEM if a is group_ids else pltpu.VMEM)(a.shape, a.dtype) for a in inputs
        ] + [
            tile,
            tile,
            pltpu.VMEM((across, DEPTH, CORES, width, seq_rows), BF16),
            tile,
            tile,
            tile,
            tile,
            pltpu.VMEM((column * lanes, groups // lanes * DEPTH, seq_rows), F32),
            pltpu.VMEM((column * lanes, groups // lanes * DEPTH, seq_rows), F32),
            pltpu.VMEM((8 * DEPTH, seq_rows), F32),
            pltpu.VMEM((DEPTH, 8, seq_rows), F32),
            pltpu.VMEM((HALF * width, SPAN), F32),
            pltpu.VMEM((width, HALF, SPAN), F32),
            pltpu.VMEM((HALF, width * SPAN), BF16),
            pltpu.VMEM((2 * width * KEPT, 2 * SPAN), BF16),
            pltpu.VMEM((width, KEPT, 2 * SPAN), F32),
            pltpu.VMEM((2 * groups, KEPT, 2 * SPAN), F32),
            pltpu.VMEM((width, KEPT, 2 * SPAN), F32),
            pltpu.VMEM((groups * KEPT, 2 * SPAN), BF16),
            pltpu.SemaphoreType.DMA((7,)),
            pltpu.SemaphoreType.DMA((7,)),
            pltpu.SemaphoreType.DMA((len(inputs),)),
        ],
        compiler_params=pltpu.CompilerParams(
            collective_id=0, has_side_effects=True, vmem_limit_bytes=67043328
        ),
    )(*inputs)
    return (output_mix, curved.T)


def solution(mesh):
    return jax.shard_map(
        local,
        mesh=mesh,
        in_specs=(
            P("seq", "chan"),
            P("seq", "chan"),
            P("seq", "chan"),
            P("seq", None),
            P("seq", None),
            P("chan"),
        ),
        out_specs=(P("seq", "chan"), P("seq", "chan")),
        check_vma=False,
    )
```

```python
import math

import jax
import jax.numpy as jnp
import numpy as np
from jax import lax
from jax.experimental import pallas as pl
from jax.experimental.pallas import tpu as pltpu
from jax.sharding import PartitionSpec as P

SPAN = 128
HALF = 64
KEPT = 80
BF16 = jnp.bfloat16
F32 = jnp.float32
MESH = pl.DeviceIdType.MESH
DEPTH = 8
CORES = 2


def tables():
    total = SPAN * SPAN
    k2 = np.arange(KEPT)
    live = (k2 <= SPAN // 2).astype(np.float64)
    n1 = np.arange(HALF)
    outer = 2 * np.pi * (np.outer(k2, n1) % SPAN) / SPAN
    enter = np.concatenate([np.cos(outer) * live[:, None], -np.sin(outer) * live[:, None]])
    weight = live * np.where((k2 == 0) | (k2 == SPAN // 2), 1.0, 2.0)
    leave = np.concatenate([(np.cos(outer) * weight[:, None]).T, (-np.sin(outer) * weight[:, None]).T], axis=1)
    fine = np.arange(SPAN)
    twist = 2 * np.pi * np.outer(k2, fine) / total
    turn = np.concatenate([np.cos(twist), np.sin(twist)], axis=1)
    inner = 2 * np.pi * (np.outer(fine, fine) % SPAN) / SPAN
    cos, sin = np.cos(inner), np.sin(inner)
    ahead = np.block([[cos, -sin], [sin, cos]])
    back = np.block([[cos, sin], [-sin, cos]])
    cast = lambda a: a.astype(np.float32).astype(BF16)
    return cast(enter), cast(leave), turn.astype(np.float32), cast(ahead), cast(back)


def dot(a, b):
    return jnp.dot(a, b, preferred_element_type=F32)


def spread_columns(src, width, wide, cols):
    wide[...] = src[...].astype(F32).reshape(HALF * width, SPAN)
    for c in range(width):
        cols[:, c * SPAN : (c + 1) * SPAN] = wide[pl.ds(c, HALF, stride=width), :].astype(BF16)


def forward(cols, enter, turn, ahead, rows, spec):
    width = spec.shape[0]
    tc, ts = turn[:, :SPAN], turn[:, SPAN:]
    for q in range(0, width, 4):
        mixed = dot(enter[...], cols[:, q * SPAN : (q + 4) * SPAN])
        for c in range(4):
            re = mixed[:KEPT, c * SPAN : (c + 1) * SPAN]
            im = mixed[KEPT:, c * SPAN : (c + 1) * SPAN]
            r0 = (q + c) * KEPT
            rows[r0 : r0 + KEPT, :SPAN] = (re * tc + im * ts).astype(BF16)
            rows[r0 : r0 + KEPT, SPAN:] = (im * tc - re * ts).astype(BF16)
    for q in range(0, width, 4):
        spec[q : q + 4] = dot(rows[q * KEPT : (q + 4) * KEPT, :], ahead[...]).reshape(4, KEPT, 2 * SPAN)


def untwist(block, tc, ts):
    re, im = block[:, :SPAN], block[:, SPAN:]
    return jnp.concatenate([re * tc - im * ts, im * tc + re * ts], axis=0).astype(BF16)


def tiles_of(block):
    return block.astype(F32).T.astype(BF16)


def body(signal_hbm, gate_hbm, curvature_hbm, filters_hbm, probe_hbm, gid_hbm,
         enter_hbm, leave_hbm, regroup_hbm, turn_hbm, ahead_hbm, back_hbm, gated, curved,
         signal, gate, curvature, filters, probe, gid, enter, leave, regroup, turn, ahead, back,
         sig_out, sig_in, tap_in, mix_out, mix_in, prim_out, home, part_out, part_in, sum_out, sum_in,
         wide, tang, cols, rows, sig_spec, tap_spec, back_spec, group_spec, send, recv, load):
    me = lax.axis_index("seq")
    lane = lax.axis_index("chan")
    peers = lax.axis_size("seq")
    lanes = lax.axis_size("chan")
    near_z, near_x = me // CORES % DEPTH, me // (CORES * DEPTH)
    core = me % CORES
    across = peers // (CORES * DEPTH)
    column = across * CORES
    width = sig_in.shape[1]
    chans = width * peers
    groups = filters.shape[0]
    total = SPAN * SPAN
    probe_scale = 1.0 / math.sqrt(HALF * SPAN)

    def seq_of(x, z, half):
        return (x * DEPTH + z) * CORES + half

    loads = [
        pltpu.make_async_copy(src, dst, load.at[i])
        for i, (src, dst) in enumerate([
            (signal_hbm, signal), (filters_hbm, filters), (probe_hbm, probe), (gate_hbm, gate),
            (curvature_hbm, curvature), (enter_hbm, enter), (turn_hbm, turn), (ahead_hbm, ahead),
            (back_hbm, back), (leave_hbm, leave), (regroup_hbm, regroup), (gid_hbm, gid),
        ])
    ]
    for copy in loads:
        copy.start()

    barrier = pltpu.get_barrier_semaphore()

    @pl.loop(1, peers)
    def _(k):
        pl.semaphore_signal(barrier, inc=1, device_id={"seq": lax.rem(me + k, peers)}, device_id_type=MESH)

    def mate(k):
        x = lax.rem(near_x + k // CORES, across)
        return seq_of(x, near_z, lax.rem(core + k, CORES))

    @pl.loop(column, column * lanes)
    def _(k):
        to = {"seq": mate(k % column), "chan": lax.rem(lane + k // column, lanes)}
        pl.semaphore_signal(barrier, inc=1, device_id=to, device_id_type=MESH)

    per = SPAN // width
    loads[0].wait()
    for b in range(chans // SPAN):
        sig_out[b * per : (b + 1) * per] = tiles_of(signal[:, b * SPAN : (b + 1) * SPAN]).reshape(per, width, SPAN)
    sig_in[me] = sig_out[me]
    loads[1].wait()
    loads[2].wait()
    signs = 2.0 * probe[...].astype(F32) - 1.0
    tap_in[near_x, near_z, core] = jnp.concatenate([filters[...].astype(F32), signs], axis=0).astype(BF16)
    loads[3].wait()
    loads[4].wait()
    for b in range(chans // SPAN):
        g32 = gate[:, b * SPAN : (b + 1) * SPAN].astype(F32)
        mixed = g32 * g32 * curvature[:, b * SPAN : (b + 1) * SPAN].astype(F32)
        mix_out[b * per : (b + 1) * per] = tiles_of(mixed).reshape(per, width, SPAN)
    mix_in[me] = mix_out[me]
    pl.semaphore_wait(barrier, peers - 1 + column * (lanes - 1))

    def put(slot, src, dst, to):
        return pltpu.make_async_remote_copy(
            src_ref=src, dst_ref=dst, send_sem=send.at[slot], recv_sem=recv.at[slot],
            device_id=to, device_id_type=MESH,
        )

    def scatter(slot, out, into):
        @pl.loop(0, peers - 1)
        def _(k):
            rank = k % DEPTH
            far = DEPTH // 2 - (rank + 1) // 2
            z = lax.rem(near_z + jnp.where(rank % 2 == 1, far, DEPTH - far), DEPTH)
            rest = (k // DEPTH + rank + 2 + DEPTH * (column - 1)) % column
            x = lax.rem(near_x + rest // CORES, across)
            to = seq_of(x, z, lax.rem(core + rest, CORES))
            put(slot, out.at[to], into.at[me], {"seq": to}).start()

    def lot(slot, ref, count):
        part = ref.at[pl.ds(0, count)]
        return put(slot, part, part, {"seq": lax.rem(me + 1, peers)})

    own_tap = tap_in.at[near_x, near_z, core]

    @pl.loop(1, DEPTH)
    def _(k):
        put(0, own_tap, own_tap, {"seq": seq_of(near_x, lax.rem(near_z + k, DEPTH), core)}).start()

    scatter(2, sig_out, sig_in)
    lot(0, sig_in, DEPTH - 1).wait_recv()
    own_line = tap_in.at[near_x, :, core]

    @pl.loop(1, column)
    def _(k):
        put(1, own_line, own_line, {"seq": mate(k)}).start()

    scatter(3, mix_out, mix_in)
    for copy in loads[5:]:
        copy.wait()
    tc, ts = turn[:, :SPAN], turn[:, SPAN:]

    lot(1, sig_in, DEPTH * (column - 1)).wait_recv()
    spread_columns(tap_in, width, wide, cols)
    forward(cols, enter, turn, ahead, rows, tap_spec)
    lot(2, sig_in, peers - 1).wait_recv()
    spread_columns(sig_in, width, wide, cols)
    forward(cols, enter, turn, ahead, rows, sig_spec)
    for c in range(width):
        g = gid[me * width + c]
        sr, si = sig_spec[c, :, :SPAN], sig_spec[c, :, SPAN:]
        for kind in range(2):
            taps = tap_spec[g + kind * groups]
            fr, fi = taps[:, :SPAN], taps[:, SPAN:]
            r0 = (2 * c + kind) * KEPT
            rows[r0 : r0 + KEPT, :SPAN] = (sr * fr - si * fi).astype(BF16)
            rows[r0 : r0 + KEPT, SPAN:] = (sr * fi + si * fr).astype(BF16)
        inner = dot(rows[2 * c * KEPT : 2 * (c + 1) * KEPT, :], back[...])
        both = jnp.concatenate([untwist(inner[:KEPT], tc, ts), untwist(inner[KEPT:], tc, ts)], axis=1)
        timed = dot(leave[...], both)
        wide[pl.ds(c, HALF, stride=width), :] = timed[:, :SPAN] * (1.0 / total)
        tang[c] = timed[:, SPAN:] * (probe_scale / total)
    prim_out[...] = wide[...].astype(BF16).reshape(prim_out.shape)
    home[me] = prim_out[me]
    scatter(4, prim_out, home)

    lot(3, mix_in, peers - 1).wait_recv()
    wide[...] = mix_in[...].astype(F32).reshape(HALF * width, SPAN)
    for c in range(width):
        tangent = tang[c].astype(BF16).astype(F32)
        cols[:, c * SPAN : (c + 1) * SPAN] = (tangent * wide[pl.ds(c, HALF, stride=width), :]).astype(BF16)
    forward(cols, enter, turn, ahead, rows, back_spec)
    for c in range(width):
        sr, si = sig_spec[c, :, :SPAN], sig_spec[c, :, SPAN:]
        br, bi = back_spec[c, :, :SPAN], back_spec[c, :, SPAN:]
        back_spec[c] = jnp.concatenate([sr * br + si * bi, sr * bi - si * br], axis=1)
    for g in range(groups):
        acc = jnp.zeros((KEPT, 2 * SPAN), F32)
        for c in range(width):
            acc = acc + jnp.where(gid[me * width + c] == g, 1.0, 0.0).astype(F32) * back_spec[c]
        group_spec[g * KEPT : (g + 1) * KEPT, :] = acc.astype(BF16)
    share = groups // lanes
    for g in range(0, groups, share):
        inner = dot(group_spec[g * KEPT : (g + share) * KEPT, :], back[...])
        both = jnp.concatenate([untwist(inner[i * KEPT : (i + 1) * KEPT], tc, ts) for i in range(share)], axis=1)
        timed = dot(regroup[...], both)
        parts = [timed[:, i * SPAN : (i + 1) * SPAN].reshape(column, DEPTH, SPAN) for i in range(share)]
        part_out[g // share * column : (g // share + 1) * column] = jnp.concatenate(parts, axis=1).astype(BF16)
    mine = lane * column + near_x * CORES + core
    part_in[mine] = part_out[mine]

    @pl.loop(1, column * lanes)
    def _(k):
        seq, chan = mate(k % column), lax.rem(lane + k // column, lanes)
        slot = chan * column + (seq // (CORES * DEPTH)) * CORES + seq % CORES
        put(5, part_out.at[slot], part_in.at[mine], {"seq": seq, "chan": chan}).start()

    lot(5, part_in, column * lanes - 1).wait_recv()
    summed = jnp.sum(part_in[...].astype(F32), axis=0)
    sum_out[...] = jnp.zeros_like(sum_out)
    for i in range(share):
        sum_out[pl.ds(i, DEPTH, stride=8), :] = summed[i * DEPTH : (i + 1) * DEPTH]
    sum_in[near_z] = sum_out[pl.ds(pl.multiple_of(near_z * 8, 8), 8), :]

    @pl.loop(1, DEPTH)
    def _(k):
        z = lax.rem(near_z + k, DEPTH)
        src = sum_out.at[pl.ds(pl.multiple_of(z * 8, 8), 8)]
        put(6, src, sum_in.at[near_z], {"seq": seq_of(near_x, z, core)}).start()

    lot(4, home, peers - 1).wait_recv()
    for b in range(chans // SPAN):
        block = home[b * per : (b + 1) * per].reshape(SPAN, SPAN)
        span = slice(b * SPAN, (b + 1) * SPAN)
        gated[:, span] = (gate[:, span].astype(F32) * block.astype(F32).T).astype(BF16)

    lot(0, sig_out, DEPTH - 1).wait_send()
    lot(1, sig_out, DEPTH * (column - 1)).wait_send()
    lot(2, sig_out, peers - 1).wait_send()
    lot(3, mix_out, peers - 1).wait_send()
    lot(4, prim_out, peers - 1).wait_send()
    lot(5, part_out, column * lanes - 1).wait_send()
    lot(6, sum_in, DEPTH - 1).wait()
    scale = 1.0 / (math.sqrt(HALF * SPAN * chans * lanes / groups) * total)
    curved[...] = (jnp.sum(sum_in[...], axis=0)[:share] * scale).astype(BF16)


def local(signal, gate, curvature, filters, probe, group_ids):
    peers, lanes = lax.axis_size("seq"), lax.axis_size("chan")
    seq_rows, chans = signal.shape
    groups = filters.shape[1]
    width = chans // peers
    across = peers // (CORES * DEPTH)
    column = across * CORES
    vmem = pl.BlockSpec(memory_space=pltpu.VMEM)
    hbm = pl.BlockSpec(memory_space=pltpu.HBM)
    tile = pltpu.VMEM((peers, width, seq_rows), BF16)
    inputs = [signal, gate, curvature, filters.T, probe.T, group_ids]
    enter, leave, turn, ahead, back = tables()
    order = np.arange(peers).reshape(across, DEPTH, CORES).transpose(0, 2, 1).reshape(-1)
    inputs += [jnp.asarray(t) for t in (enter, leave, leave[order], turn, ahead, back)]
    output_mix, curved = pl.pallas_call(
        body,
        out_shape=(
            jax.ShapeDtypeStruct((seq_rows, chans), BF16),
            jax.ShapeDtypeStruct((groups // lanes, seq_rows), BF16),
        ),
        in_specs=[hbm] * len(inputs),
        out_specs=(vmem, vmem),
        scratch_shapes=[
            (pltpu.SMEM if a is group_ids else pltpu.VMEM)(a.shape, a.dtype) for a in inputs
        ] + [
            tile,
            tile,
            pltpu.VMEM((across, DEPTH, CORES, width, seq_rows), BF16),
            tile,
            tile,
            tile,
            tile,
            pltpu.VMEM((column * lanes, groups // lanes * DEPTH, seq_rows), BF16),
            pltpu.VMEM((column * lanes, groups // lanes * DEPTH, seq_rows), BF16),
            pltpu.VMEM((8 * DEPTH, seq_rows), F32),
            pltpu.VMEM((DEPTH, 8, seq_rows), F32),
            pltpu.VMEM((HALF * width, SPAN), F32),
            pltpu.VMEM((width, HALF, SPAN), F32),
            pltpu.VMEM((HALF, width * SPAN), BF16),
            pltpu.VMEM((2 * width * KEPT, 2 * SPAN), BF16),
            pltpu.VMEM((width, KEPT, 2 * SPAN), F32),
            pltpu.VMEM((2 * groups, KEPT, 2 * SPAN), F32),
            pltpu.VMEM((width, KEPT, 2 * SPAN), F32),
            pltpu.VMEM((groups * KEPT, 2 * SPAN), BF16),
            pltpu.SemaphoreType.DMA((7,)),
            pltpu.SemaphoreType.DMA((7,)),
            pltpu.SemaphoreType.DMA((len(inputs),)),
        ],
        compiler_params=pltpu.CompilerParams(
            collective_id=0, has_side_effects=True, vmem_limit_bytes=67043328
        ),
    )(*inputs)
    return (output_mix, curved.T)


def solution(mesh):
    return jax.shard_map(
        local,
        mesh=mesh,
        in_specs=(
            P("seq", "chan"),
            P("seq", "chan"),
            P("seq", "chan"),
            P("seq", None),
            P("seq", None),
            P("chan"),
        ),
        out_specs=(P("seq", "chan"), P("seq", "chan")),
        check_vma=False,
    )
```

```python
import math

import jax
import jax.numpy as jnp
import numpy as np
from jax import lax
from jax.experimental import pallas as pl
from jax.experimental.pallas import tpu as pltpu
from jax.sharding import PartitionSpec as P

SPAN = 128
HALF = 64
KEPT = 80
BF16 = jnp.bfloat16
F32 = jnp.float32
MESH = pl.DeviceIdType.MESH
DEPTH = 8
CORES = 2
VMEM_LIMIT = 16 << 20


def tables():
    total = SPAN * SPAN
    k2 = np.arange(KEPT)
    live = (k2 <= SPAN // 2).astype(np.float64)
    n1 = np.arange(HALF)
    outer = 2 * np.pi * (np.outer(k2, n1) % SPAN) / SPAN
    enter = np.concatenate([np.cos(outer) * live[:, None], -np.sin(outer) * live[:, None]])
    weight = live * np.where((k2 == 0) | (k2 == SPAN // 2), 1.0, 2.0)
    leave = np.concatenate([(np.cos(outer) * weight[:, None]).T, (-np.sin(outer) * weight[:, None]).T], axis=1)
    fine = np.arange(SPAN)
    twist = 2 * np.pi * np.outer(k2, fine) / total
    turn = np.concatenate([np.cos(twist), np.sin(twist)], axis=1)
    inner = 2 * np.pi * (np.outer(fine, fine) % SPAN) / SPAN
    cos, sin = np.cos(inner), np.sin(inner)
    ahead = np.block([[cos, -sin], [sin, cos]])
    back = np.block([[cos, sin], [-sin, cos]])
    cast = lambda a: a.astype(np.float32).astype(BF16)
    return cast(enter), cast(leave), turn.astype(np.float32), cast(ahead), cast(back)


def dot(a, b):
    return jnp.dot(a, b, preferred_element_type=F32)


def spread_columns(src, width, wide, cols):
    wide[...] = src[...].astype(F32).reshape(HALF * width, SPAN)
    for c in range(width):
        cols[:, c * SPAN : (c + 1) * SPAN] = wide[pl.ds(c, HALF, stride=width), :].astype(BF16)


def forward(cols, enter, turn, ahead, rows, spec):
    width = spec.shape[0]
    tc, ts = turn[:, :SPAN], turn[:, SPAN:]
    for q in range(0, width, 4):
        mixed = dot(enter[...], cols[:, q * SPAN : (q + 4) * SPAN])
        for c in range(4):
            re = mixed[:KEPT, c * SPAN : (c + 1) * SPAN]
            im = mixed[KEPT:, c * SPAN : (c + 1) * SPAN]
            r0 = (q + c) * KEPT
            rows[r0 : r0 + KEPT, :SPAN] = (re * tc + im * ts).astype(BF16)
            rows[r0 : r0 + KEPT, SPAN:] = (im * tc - re * ts).astype(BF16)
    for q in range(0, width, 4):
        spec[q : q + 4] = dot(rows[q * KEPT : (q + 4) * KEPT, :], ahead[...]).reshape(4, KEPT, 2 * SPAN)


def untwist(block, tc, ts):
    re, im = block[:, :SPAN], block[:, SPAN:]
    return jnp.concatenate([re * tc - im * ts, im * tc + re * ts], axis=0).astype(BF16)


def tiles_of(block):
    return block.astype(F32).T.astype(BF16)


def body(signal_hbm, gate_hbm, curvature_hbm, filters_hbm, probe_hbm, gid_hbm,
         enter_hbm, leave_hbm, regroup_hbm, turn_hbm, ahead_hbm, back_hbm, gated, curved,
         signal, gate, curvature, filters, probe, gid, enter, leave, regroup, turn, ahead, back,
         sig_out, sig_in, tap_in, mix_out, mix_in, prim_out, home, part_out, part_in, sum_out, sum_in,
         wide, tang, cols, rows, sig_spec, tap_spec, back_spec, group_spec, send, recv, load):
    me = lax.axis_index("seq")
    lane = lax.axis_index("chan")
    peers = lax.axis_size("seq")
    lanes = lax.axis_size("chan")
    near_z, near_x = me // CORES % DEPTH, me // (CORES * DEPTH)
    core = me % CORES
    across = peers // (CORES * DEPTH)
    column = across * CORES
    width = sig_in.shape[1]
    chans = width * peers
    groups = filters.shape[0]
    total = SPAN * SPAN
    probe_scale = 1.0 / math.sqrt(HALF * SPAN)

    def seq_of(x, z, half):
        return (x * DEPTH + z) * CORES + half

    loads = [
        pltpu.make_async_copy(src, dst, load.at[i])
        for i, (src, dst) in enumerate([
            (signal_hbm, signal), (filters_hbm, filters), (probe_hbm, probe), (gate_hbm, gate),
            (curvature_hbm, curvature), (enter_hbm, enter), (turn_hbm, turn), (ahead_hbm, ahead),
            (back_hbm, back), (leave_hbm, leave), (regroup_hbm, regroup), (gid_hbm, gid),
        ])
    ]
    for copy in loads:
        copy.start()

    barrier = pltpu.get_barrier_semaphore()

    @pl.loop(1, peers)
    def _(k):
        pl.semaphore_signal(barrier, inc=1, device_id={"seq": lax.rem(me + k, peers)}, device_id_type=MESH)

    def mate(k):
        x = lax.rem(near_x + k // CORES, across)
        return seq_of(x, near_z, lax.rem(core + k, CORES))

    @pl.loop(column, column * lanes)
    def _(k):
        to = {"seq": mate(k % column), "chan": lax.rem(lane + k // column, lanes)}
        pl.semaphore_signal(barrier, inc=1, device_id=to, device_id_type=MESH)

    per = SPAN // width
    loads[0].wait()
    for b in range(chans // SPAN):
        sig_out[b * per : (b + 1) * per] = tiles_of(signal[:, b * SPAN : (b + 1) * SPAN]).reshape(per, width, SPAN)
    sig_in[me] = sig_out[me]
    loads[1].wait()
    loads[2].wait()
    signs = 2.0 * probe[...].astype(F32) - 1.0
    tap_in[near_x, near_z, core] = jnp.concatenate([filters[...].astype(F32), signs], axis=0).astype(BF16)
    pl.semaphore_wait(barrier, peers - 1 + column * (lanes - 1))

    def put(slot, src, dst, to):
        return pltpu.make_async_remote_copy(
            src_ref=src, dst_ref=dst, send_sem=send.at[slot], recv_sem=recv.at[slot],
            device_id=to, device_id_type=MESH,
        )

    def scatter(slot, out, into):
        @pl.loop(0, peers - 1)
        def _(k):
            rank = k % DEPTH
            far = DEPTH // 2 - (rank + 1) // 2
            z = lax.rem(near_z + jnp.where(rank % 2 == 1, far, DEPTH - far), DEPTH)
            rest = (k // DEPTH + rank + 2 + DEPTH * (column - 1)) % column
            x = lax.rem(near_x + rest // CORES, across)
            to = seq_of(x, z, lax.rem(core + rest, CORES))
            put(slot, out.at[to], into.at[me], {"seq": to}).start()

    def lot(slot, ref, count):
        part = ref.at[pl.ds(0, count)]
        return put(slot, part, part, {"seq": lax.rem(me + 1, peers)})

    own_tap = tap_in.at[near_x, near_z, core]

    @pl.loop(1, DEPTH)
    def _(k):
        put(0, own_tap, own_tap, {"seq": seq_of(near_x, lax.rem(near_z + k, DEPTH), core)}).start()

    scatter(2, sig_out, sig_in)
    loads[3].wait()
    loads[4].wait()
    for b in range(chans // SPAN):
        g32 = gate[:, b * SPAN : (b + 1) * SPAN].astype(F32)
        mixed = g32 * g32 * curvature[:, b * SPAN : (b + 1) * SPAN].astype(F32)
        mix_out[b * per : (b + 1) * per] = tiles_of(mixed).reshape(per, width, SPAN)
    mix_in[me] = mix_out[me]
    lot(0, sig_in, DEPTH - 1).wait_recv()
    own_line = tap_in.at[near_x, :, core]

    @pl.loop(1, column)
    def _(k):
        put(1, own_line, own_line, {"seq": mate(k)}).start()

    scatter(3, mix_out, mix_in)
    for copy in loads[5:]:
        copy.wait()
    tc, ts = turn[:, :SPAN], turn[:, SPAN:]

    lot(1, sig_in, DEPTH * (column - 1)).wait_recv()
    spread_columns(tap_in, width, wide, cols)
    forward(cols, enter, turn, ahead, rows, tap_spec)
    lot(2, sig_in, peers - 1).wait_recv()
    spread_columns(sig_in, width, wide, cols)
    forward(cols, enter, turn, ahead, rows, sig_spec)
    for c in range(width):
        g = gid[me * width + c]
        sr, si = sig_spec[c, :, :SPAN], sig_spec[c, :, SPAN:]
        for kind in range(2):
            taps = tap_spec[g + kind * groups]
            fr, fi = taps[:, :SPAN], taps[:, SPAN:]
            r0 = (2 * c + kind) * KEPT
            rows[r0 : r0 + KEPT, :SPAN] = (sr * fr - si * fi).astype(BF16)
            rows[r0 : r0 + KEPT, SPAN:] = (sr * fi + si * fr).astype(BF16)
        inner = dot(rows[2 * c * KEPT : 2 * (c + 1) * KEPT, :], back[...])
        both = jnp.concatenate([untwist(inner[:KEPT], tc, ts), untwist(inner[KEPT:], tc, ts)], axis=1)
        timed = dot(leave[...], both)
        wide[pl.ds(c, HALF, stride=width), :] = timed[:, :SPAN] * (1.0 / total)
        tang[c] = timed[:, SPAN:] * (probe_scale / total)
    prim_out[...] = wide[...].astype(BF16).reshape(prim_out.shape)
    home[me] = prim_out[me]
    scatter(4, prim_out, home)

    lot(3, mix_in, peers - 1).wait_recv()
    wide[...] = mix_in[...].astype(F32).reshape(HALF * width, SPAN)
    for c in range(width):
        tangent = tang[c].astype(BF16).astype(F32)
        cols[:, c * SPAN : (c + 1) * SPAN] = (tangent * wide[pl.ds(c, HALF, stride=width), :]).astype(BF16)
    forward(cols, enter, turn, ahead, rows, back_spec)
    for c in range(width):
        sr, si = sig_spec[c, :, :SPAN], sig_spec[c, :, SPAN:]
        br, bi = back_spec[c, :, :SPAN], back_spec[c, :, SPAN:]
        back_spec[c] = jnp.concatenate([sr * br + si * bi, sr * bi - si * br], axis=1)
    for g in range(groups):
        acc = jnp.zeros((KEPT, 2 * SPAN), F32)
        for c in range(width):
            acc = acc + jnp.where(gid[me * width + c] == g, 1.0, 0.0).astype(F32) * back_spec[c]
        group_spec[g * KEPT : (g + 1) * KEPT, :] = acc.astype(BF16)
    share = groups // lanes
    for g in range(0, groups, share):
        inner = dot(group_spec[g * KEPT : (g + share) * KEPT, :], back[...])
        both = jnp.concatenate([untwist(inner[i * KEPT : (i + 1) * KEPT], tc, ts) for i in range(share)], axis=1)
        timed = dot(regroup[...], both)
        parts = [timed[:, i * SPAN : (i + 1) * SPAN].reshape(column, DEPTH, SPAN) for i in range(share)]
        part_out[g // share * column : (g // share + 1) * column] = jnp.concatenate(parts, axis=1).astype(BF16)
    mine = lane * column + near_x * CORES + core
    part_in[mine] = part_out[mine]

    @pl.loop(1, column * lanes)
    def _(k):
        seq, chan = mate(k % column), lax.rem(lane + k // column, lanes)
        slot = chan * column + (seq // (CORES * DEPTH)) * CORES + seq % CORES
        put(5, part_out.at[slot], part_in.at[mine], {"seq": seq, "chan": chan}).start()

    lot(5, part_in, column * lanes - 1).wait_recv()
    summed = jnp.sum(part_in[...].astype(F32), axis=0)
    sum_out[...] = jnp.zeros_like(sum_out)
    for i in range(share):
        sum_out[pl.ds(i, DEPTH, stride=8), :] = summed[i * DEPTH : (i + 1) * DEPTH]
    sum_in[near_z] = sum_out[pl.ds(pl.multiple_of(near_z * 8, 8), 8), :]

    @pl.loop(1, DEPTH)
    def _(k):
        z = lax.rem(near_z + k, DEPTH)
        src = sum_out.at[pl.ds(pl.multiple_of(z * 8, 8), 8)]
        put(6, src, sum_in.at[near_z], {"seq": seq_of(near_x, z, core)}).start()

    lot(4, home, peers - 1).wait_recv()
    for b in range(chans // SPAN):
        block = home[b * per : (b + 1) * per].reshape(SPAN, SPAN)
        span = slice(b * SPAN, (b + 1) * SPAN)
        gated[:, span] = (gate[:, span].astype(F32) * block.astype(F32).T).astype(BF16)

    lot(0, sig_out, DEPTH - 1).wait_send()
    lot(1, sig_out, DEPTH * (column - 1)).wait_send()
    lot(2, sig_out, peers - 1).wait_send()
    lot(3, mix_out, peers - 1).wait_send()
    lot(4, prim_out, peers - 1).wait_send()
    lot(5, part_out, column * lanes - 1).wait_send()
    lot(6, sum_in, DEPTH - 1).wait()
    scale = 1.0 / (math.sqrt(HALF * SPAN * chans * lanes / groups) * total)
    curved[...] = (jnp.sum(sum_in[...], axis=0)[:share] * scale).astype(BF16)


def local(signal, gate, curvature, filters, probe, group_ids):
    peers, lanes = lax.axis_size("seq"), lax.axis_size("chan")
    seq_rows, chans = signal.shape
    groups = filters.shape[1]
    width = chans // peers
    across = peers // (CORES * DEPTH)
    column = across * CORES
    vmem = pl.BlockSpec(memory_space=pltpu.VMEM)
    hbm = pl.BlockSpec(memory_space=pltpu.HBM)
    tile = pltpu.VMEM((peers, width, seq_rows), BF16)
    inputs = [signal, gate, curvature, filters.T, probe.T, group_ids]
    enter, leave, turn, ahead, back = tables()
    order = np.arange(peers).reshape(across, DEPTH, CORES).transpose(0, 2, 1).reshape(-1)
    inputs += [jnp.asarray(t) for t in (enter, leave, leave[order], turn, ahead, back)]
    output_mix, curved = pl.pallas_call(
        body,
        out_shape=(
            jax.ShapeDtypeStruct((seq_rows, chans), BF16),
            jax.ShapeDtypeStruct((groups // lanes, seq_rows), BF16),
        ),
        in_specs=[hbm] * len(inputs),
        out_specs=(vmem, vmem),
        scratch_shapes=[
            (pltpu.SMEM if a is group_ids else pltpu.VMEM)(a.shape, a.dtype) for a in inputs
        ] + [
            tile,
            tile,
            pltpu.VMEM((across, DEPTH, CORES, width, seq_rows), BF16),
            tile,
            tile,
            tile,
            tile,
            pltpu.VMEM((column * lanes, groups // lanes * DEPTH, seq_rows), BF16),
            pltpu.VMEM((column * lanes, groups // lanes * DEPTH, seq_rows), BF16),
            pltpu.VMEM((8 * DEPTH, seq_rows), F32),
            pltpu.VMEM((DEPTH, 8, seq_rows), F32),
            pltpu.VMEM((HALF * width, SPAN), F32),
            pltpu.VMEM((width, HALF, SPAN), F32),
            pltpu.VMEM((HALF, width * SPAN), BF16),
            pltpu.VMEM((2 * width * KEPT, 2 * SPAN), BF16),
            pltpu.VMEM((width, KEPT, 2 * SPAN), F32),
            pltpu.VMEM((2 * groups, KEPT, 2 * SPAN), F32),
            pltpu.VMEM((width, KEPT, 2 * SPAN), F32),
            pltpu.VMEM((groups * KEPT, 2 * SPAN), BF16),
            pltpu.SemaphoreType.DMA((7,)),
            pltpu.SemaphoreType.DMA((7,)),
            pltpu.SemaphoreType.DMA((len(inputs),)),
        ],
        compiler_params=pltpu.CompilerParams(
            collective_id=0, has_side_effects=True, vmem_limit_bytes=VMEM_LIMIT
        ),
    )(*[pltpu.with_memory_space_constraint(a, pltpu.HBM) for a in inputs])
    return (output_mix, curved.T)


def solution(mesh):
    return jax.shard_map(
        local,
        mesh=mesh,
        in_specs=(
            P("seq", "chan"),
            P("seq", "chan"),
            P("seq", "chan"),
            P("seq", None),
            P("seq", None),
            P("chan"),
        ),
        out_specs=(P("seq", "chan"), P("seq", "chan")),
        check_vma=False,
    )
```
